1024 devices in a mesh: fsdp: 32 (over y_lo, z, core), head: 32 (over y_hi, x).
Axes of the slice: x: 8, y: 8 (y_hi: 4, y_lo: 2; y = y_hi * 2 + y_lo), z: 8, core: 2. Of those that a mesh axis runs over, the one named last changes fastest.
Arguments:
- tokens: bfloat16 [8192, 4096], P('fsdp'), may hold values from -6 to 6
- zx_weight: bfloat16 [4096, 128, 128], P('fsdp', 'head'), may hold values from -0.09375 to 0.09375
- dt_weight: bfloat16 [4096, 128], P('fsdp', 'head'), may hold values from -0.09375 to 0.09375
- bc_weight: bfloat16 [4096, 1024], P('fsdp'), may hold values from -0.09375 to 0.09375
- conv_x: float32 [4, 8192], P(None, 'head'), may hold values from -2 to 2
- conv_bc: float32 [4, 1024], replicated, may hold values from -2 to 2
- a_log: float32 [128], P('head'), may hold values from -5 to 0.5
- dt_bias: float32 [128], P('head'), may hold values from -4 to 0
- d_skip: float32 [128], P('head'), may hold values from 0.5 to 2
- norm_gain: float32 [8192], P('head'), may hold values from 0.1 to 1.9
- out_weight: bfloat16 [8192, 4096], P('head'), may hold values from -0.125 to 0.125
Outputs:
- mixed: bfloat16 [8192, 4096], P('fsdp', 'head')
The draws below stay inside these ranges and needn't reach their ends.
All inputs are finite; a program needn't handle non-finite values.
Results may differ from the reference program's by a relative error of at most 0.015.
Values may be sent and summed in bfloat16 or wider, within the bound.
No kernel may reach another device: no remote copies, remote signals or barrier semaphores. Data moves between devices by JAX's collectives and lax.ppermute only.
A program may use at most 32 MiB of HBM per device.

```python
import jax
import jax.numpy as jnp
from jax import lax

D = 4096
HEADS = 128
P_SIZE = 64
N = 128
G = 4
KCONV = 4
LEN = 256
INNER = 8192
TOKENS = 8192
N_HEAD = 32


def with_spikes(values, rng, source, target, parts, factor):
    owner, partner = [(jnp.arange(values.shape[position]) // (values.shape[position] // parts)).reshape([-1 if axis == position else 1 for axis in range(values.ndim)]) for position in (source, target)]
    chosen = jax.random.permutation(rng, parts)[partner]
    strong = (owner == chosen) | (owner == (partner + parts // 2) % parts)
    return jnp.where(strong, factor * values, values)


def block_scale(stream_key, shape, shards, least, largest):
    loudness = 1.0
    for position, shards_of in shards:
        steps = jax.random.uniform(jax.random.fold_in(jax.random.fold_in(stream_key, 6), position), (shards_of,), jnp.float32, least / len(shards), largest / len(shards))
        loudness = loudness * jnp.repeat(jnp.exp(steps), shape[position] // shards_of).reshape((-1,) + (1,) * (len(shape) - 1 - position))
    return loudness


def normal_values(key, shape, deviation, reach, split=(), kind=jnp.bfloat16):
    entries = deviation * jax.random.normal(key, shape, jnp.float32)
    if split:
        entries = entries * block_scale(key, shape, split, -0.22, 0.18)
    return jnp.clip(entries, -reach, reach).astype(kind)


def bell_draw_with(key, shape, width, bound, split, heavy, dtype=jnp.bfloat16):
    values = width * jax.random.normal(key, shape, jnp.float32)
    if split:
        values = values * block_scale(key, shape, split, -0.22, 0.18)
    return jnp.clip(with_spikes(values, jax.random.fold_in(key, 3), *heavy), -bound, bound).astype(dtype)


def setup_inputs(seed: int = 0) -> dict:
    arg_keys = jax.random.split(jax.random.key(seed), 12)
    return {
        "tokens": normal_values(arg_keys[0], (TOKENS, D), 1.0, 6.0, ((0, 32),)),
        "zx_weight": normal_values(arg_keys[1], (D, HEADS, 2 * P_SIZE), D ** -0.5, 0.09375, ((0, 32), (1, 32))),
        "dt_weight": normal_values(arg_keys[2], (D, HEADS), D ** -0.5, 0.09375, ((0, 32), (1, 32))),
        "bc_weight": normal_values(arg_keys[3], (D, G * 2 * N), D ** -0.5, 0.09375, ((0, 32),)),
        "conv_x": normal_values(arg_keys[4], (KCONV, INNER), 0.5, 2.0, ((1, 32),), jnp.float32),
        "conv_bc": normal_values(arg_keys[5], (KCONV, G * 2 * N), 0.5, 2.0, (), jnp.float32),
        "a_log": jnp.clip(-5.0 + 5.5 * jax.random.uniform(arg_keys[6], (HEADS,), jnp.float32) ** block_scale(arg_keys[6], (HEADS,), ((0, 32),), -0.2, 0.2), -5.0, 0.5),
        "dt_bias": jnp.clip(-4.0 + 4.0 * jax.random.uniform(arg_keys[7], (HEADS,), jnp.float32) ** block_scale(arg_keys[7], (HEADS,), ((0, 32),), -0.2, 0.2), -4.0, 0.0),
        "d_skip": jnp.clip(0.5 + 1.5 * jax.random.uniform(arg_keys[8], (HEADS,), jnp.float32) ** block_scale(arg_keys[8], (HEADS,), ((0, 32),), -0.2, 0.2), 0.5, 2.0),
        "norm_gain": jnp.clip(1.0 + 0.18 * jax.random.normal(arg_keys[9], (INNER,), jnp.float32), 0.1, 1.9),
        "out_weight": bell_draw_with(arg_keys[10], (INNER, D), INNER ** -0.5, 0.125, ((0, 32),), (0, 1, 32, 2.75)),
    }


def settle(values):
    return lax.optimization_barrier(values.astype(jnp.bfloat16))

def causal(values, kernel):
    columns = values.shape[1]
    seqs = values.reshape(-1, LEN, columns).astype(jnp.float32)
    padded = jnp.pad(seqs, ((0, 0), (KCONV - 1, 0), (0, 0)))
    total = jnp.zeros(seqs.shape, jnp.float32)
    for tap in range(KCONV):
        total = total + kernel[tap].astype(jnp.float32) * padded[:, tap:tap + LEN]
    return settle(jax.nn.silu(total).reshape(-1, columns))

def reference(tokens, zx_weight, dt_weight, bc_weight, conv_x, conv_bc, a_log, dt_bias, d_skip, norm_gain, out_weight):
    flat = zx_weight.reshape(D, HEADS * 2 * P_SIZE)
    zx = settle(jnp.dot(tokens, flat, preferred_element_type=jnp.float32)).reshape(TOKENS, HEADS, 2, P_SIZE)
    gate = zx[:, :, 0, :].astype(jnp.float32).reshape(TOKENS, INNER)
    xin = zx[:, :, 1, :].reshape(TOKENS, INNER)
    dt_raw = settle(jnp.dot(tokens, dt_weight, preferred_element_type=jnp.float32))
    bc_raw = settle(jnp.dot(tokens, bc_weight, preferred_element_type=jnp.float32))
    xconv = causal(xin, conv_x)
    bconv = causal(bc_raw, conv_bc).reshape(TOKENS, G, 2, N)
    steps = jax.nn.softplus(dt_raw.astype(jnp.float32) + dt_bias)
    rates = jnp.exp(a_log)
    count = TOKENS // LEN
    xs = xconv.astype(jnp.float32).reshape(count, LEN, HEADS, P_SIZE)
    bs = bconv[:, :, 0, :].astype(jnp.float32).reshape(count, LEN, G, N)
    cs = bconv[:, :, 1, :].astype(jnp.float32).reshape(count, LEN, G, N)
    ds = steps.reshape(count, LEN, HEADS)
    lower = jnp.arange(LEN)[:, None] >= jnp.arange(LEN)[None, :]

    def one(item):
        xval, bval, cval, dval = item
        cum = jnp.cumsum(-dval * rates, axis=0)
        seg = cum[:, None, :] - cum[None, :, :]
        decay = jnp.exp(jnp.where(lower[:, :, None], seg, -1e+30))
        inner = jnp.einsum('tgn,sgn->gts', cval, bval, precision=lax.Precision.HIGHEST)
        inner = jnp.repeat(inner, HEADS // G, axis=0).transpose(1, 2, 0)
        weights = inner * decay * dval[None, :, :]
        out = jnp.einsum('tsh,shp->thp', weights, xval, precision=lax.Precision.HIGHEST)
        return out + d_skip[None, :, None] * xval
    ys = lax.map(one, (xs, bs, cs, ds)).reshape(TOKENS, INNER)
    gated = ys * jax.nn.silu(gate)
    grouped = gated.reshape(TOKENS, G, INNER // G)
    meansq = lax.optimization_barrier(jnp.mean(grouped * grouped, axis=2, keepdims=True))
    normed = (grouped / jnp.sqrt(meansq + 1e-05)).reshape(TOKENS, INNER) * norm_gain
    normed = normed.astype(jnp.bfloat16)
    block = INNER // N_HEAD

    def accumulate(index, total):
        left = lax.dynamic_slice_in_dim(normed, index * block, block, 1)
        right = lax.dynamic_slice_in_dim(out_weight, index * block, block, 0)
        part = settle(jnp.dot(left, right, preferred_element_type=jnp.float32))
        return total + part.astype(jnp.float32)
    total = lax.fori_loop(0, N_HEAD, accumulate, jnp.zeros((TOKENS, D), jnp.float32))
    return total.astype(jnp.bfloat16)
```

```python
import jax
import jax.numpy as jnp
from jax import lax
from jax.sharding import Mesh, PartitionSpec as P

LEN = 256
FSDP = ("yl", "z", "core")
HEAD = ("yh", "x")
SIZES = (2, 8, 2, 4, 8)


def settle(values):
    return lax.optimization_barrier(values.astype(jnp.bfloat16))


def causal(values, kernel, seq_len):
    columns = values.shape[1]
    seqs = values.reshape(-1, seq_len, columns).astype(jnp.float32)
    taps = kernel.shape[0]
    padded = jnp.pad(seqs, ((0, 0), (taps - 1, 0), (0, 0)))
    total = jnp.zeros(seqs.shape, jnp.float32)
    for tap in range(taps):
        total = total + kernel[tap] * padded[:, tap : tap + seq_len]
    return settle(jax.nn.silu(total).reshape(-1, columns))


def on_device(
    tokens,
    zx_weight,
    dt_weight,
    bc_weight,
    conv_x,
    conv_bc,
    a_log,
    dt_bias,
    d_skip,
    norm_gain,
    out_weight,
):
    f32, bf16 = jnp.float32, jnp.bfloat16
    tok_rows = tokens.shape[0]
    rows, heads_here, two_p = zx_weight.shape
    head_size = two_p // 2
    channels = heads_here * head_size
    n_yh, n_x = lax.axis_size("yh"), lax.axis_size("x")
    group_id = lax.axis_index("yh")
    group_cols = bc_weight.shape[1] // n_yh
    state = group_cols // 2
    bc_part = lax.dynamic_slice_in_dim(bc_weight, group_id * group_cols, group_cols, 1)
    zx_cols = heads_here * two_p
    pad = -(zx_cols + group_cols + heads_here) % 128
    mine = jnp.concatenate(
        [
            zx_weight.reshape(rows, zx_cols),
            bc_part,
            dt_weight,
            jnp.zeros((rows, pad), bf16),
        ],
        axis=1,
    )
    whole = lax.all_gather(mine, FSDP, axis=0, tiled=True)

    width = out_weight.shape[1] // (n_yh * n_x)
    scaled = (out_weight.astype(f32) * norm_gain[:, None]).astype(bf16)
    pieces = scaled.reshape(channels, n_yh, n_x, width).transpose(2, 0, 1, 3)
    pieces = pieces.reshape(n_x, channels, n_yh * width)
    group_weight = lax.all_to_all(pieces, "x", 0, 0).reshape(n_x * channels, n_yh * width)

    whole, group_weight = lax.optimization_barrier((whole, group_weight))
    acc = jnp.dot(tokens, whole, preferred_element_type=f32)
    acc = settle(acc)
    zx = acc[:, :zx_cols].reshape(tok_rows, heads_here, 2, head_size)
    bc_raw = acc[:, zx_cols : zx_cols + group_cols]
    dt_raw = acc[:, zx_cols + group_cols : zx_cols + group_cols + heads_here]
    gate = zx[:, :, 0, :].astype(f32).reshape(tok_rows, channels)
    xin = zx[:, :, 1, :].reshape(tok_rows, channels)
    xconv = causal(xin, conv_x, LEN)
    conv_group = lax.dynamic_slice_in_dim(conv_bc, group_id * group_cols, group_cols, 1)
    bconv = causal(bc_raw, conv_group, LEN)
    count = tok_rows // LEN
    steps = jax.nn.softplus(dt_raw.astype(f32) + dt_bias).reshape(count, LEN, heads_here)
    cum = jnp.cumsum(-steps * jnp.exp(a_log), axis=1)
    seg = cum[:, :, None, :] - cum[:, None, :, :]
    lower = jnp.arange(LEN)[:, None] >= jnp.arange(LEN)[None, :]
    decay = jnp.exp(jnp.where(lower[None, :, :, None], seg, -1e30))
    bseq = bconv[:, :state].reshape(count, LEN, state)
    cseq = bconv[:, state:].reshape(count, LEN, state)
    inner = jnp.einsum("btn,bsn->bts", cseq, bseq, preferred_element_type=f32)
    weights = inner[..., None] * decay * steps[:, None, :, :]
    xval = xconv.astype(f32).reshape(count, LEN, heads_here, head_size)
    ys = jnp.einsum("btsh,bshp->bthp", weights, xval, precision=lax.Precision.HIGHEST)
    ys = ys + d_skip[None, None, :, None] * xval
    gated = (ys.reshape(tok_rows, channels) * jax.nn.silu(gate)).astype(bf16)

    spread = jnp.broadcast_to(gated[None], (n_x, tok_rows, channels))
    group = lax.all_to_all(spread, "x", 0, 0)
    squares = jnp.sum(jnp.square(group.astype(f32)), axis=(0, 2))
    scale = lax.rsqrt(squares / (n_x * channels) + 1e-05)
    parts = jnp.einsum(
        "xtc,xcyw->ytw",
        group,
        group_weight.reshape(n_x, channels, n_yh, width),
        preferred_element_type=f32,
    )
    parts = (parts * scale[None, :, None]).astype(bf16)
    got = lax.all_to_all(parts, "yh", 0, 0)
    return jnp.sum(got.astype(f32), axis=0).astype(bf16)


def solution(mesh):
    fine = Mesh(mesh.devices.reshape(SIZES), FSDP + HEAD)
    in_specs = (
        P(FSDP, None),
        P(FSDP, HEAD, None),
        P(FSDP, HEAD),
        P(FSDP, None),
        P(None, HEAD),
        P(),
        P(HEAD),
        P(HEAD),
        P(HEAD),
        P(HEAD),
        P(HEAD, None),
    )
    return jax.shard_map(
        on_device, mesh=fine, in_specs=in_specs, out_specs=P(FSDP, HEAD), check_vma=False
    )
```

```python
import jax
import jax.numpy as jnp
from jax import lax
from jax.experimental import pallas as pl
from jax.sharding import Mesh, PartitionSpec as P

LEN = 256
FSDP = ("yl", "z", "core")
HEAD = ("yh", "x")
SIZES = (2, 8, 2, 4, 8)
SWAP = [(0, 1), (1, 0)]


def repack(weight, gain, n_yh, n_x):
    rows, columns = weight.shape
    width = columns // (n_yh * n_x)

    def kernel(gain_ref, *refs):
        out_ref = refs[-1]
        for i, ref in enumerate(refs[:-1]):
            value = ref[...].astype(jnp.float32) * gain_ref[...]
            out_ref[0, :, i * width : (i + 1) * width] = value.astype(jnp.bfloat16)

    def spec(i):
        return pl.BlockSpec((rows, width), lambda x: (0, i * n_x + x))

    return pl.pallas_call(
        kernel,
        grid=(n_x,),
        in_specs=[pl.BlockSpec((rows, 1), lambda x: (0, 0))] + [spec(i) for i in range(n_yh)],
        out_specs=pl.BlockSpec((1, rows, n_yh * width), lambda x: (x, 0, 0)),
        out_shape=jax.ShapeDtypeStruct((n_x, rows, n_yh * width), jnp.bfloat16),
        cost_estimate=pl.CostEstimate(
            flops=rows * columns, bytes_accessed=4 * rows * columns, transcendentals=0
        ),
        name="repack",
    )(gain[:, None], *[weight] * n_yh)


def settle(values):
    return lax.optimization_barrier(values.astype(jnp.bfloat16))


def causal(values, kernel, seq_len):
    columns = values.shape[1]
    seqs = values.reshape(-1, seq_len, columns).astype(jnp.float32)
    taps = kernel.shape[0]
    padded = jnp.pad(seqs, ((0, 0), (taps - 1, 0), (0, 0)))
    total = jnp.zeros(seqs.shape, jnp.float32)
    for tap in range(taps):
        total = total + kernel[tap] * padded[:, tap : tap + seq_len]
    return settle(jax.nn.silu(total).reshape(-1, columns))


def layer(
    tokens,
    zx_weight,
    dt_weight,
    bc_weight,
    conv_x,
    conv_bc,
    a_log,
    dt_bias,
    d_skip,
    norm_gain,
    out_weight,
):
    f32, bf16 = jnp.float32, jnp.bfloat16
    tok_rows = tokens.shape[0]
    rows, heads_here, two_p = zx_weight.shape
    head_size = two_p // 2
    channels = heads_here * head_size
    n_yh, n_x = lax.axis_size("yh"), lax.axis_size("x")
    group_id = lax.axis_index("yh")
    group_cols = bc_weight.shape[1] // n_yh
    state = group_cols // 2
    bc_part = lax.dynamic_slice_in_dim(bc_weight, group_id * group_cols, group_cols, 1)
    zx_cols = heads_here * two_p
    pad = -(zx_cols + group_cols + heads_here) % 128
    mine = jnp.concatenate(
        [
            zx_weight.reshape(rows, zx_cols),
            bc_part,
            dt_weight,
            jnp.zeros((rows, pad), bf16),
        ],
        axis=1,
    )
    k_half, z_pos, c_pos = lax.axis_index("yl"), lax.axis_index("z"), lax.axis_index("core")
    n_z = lax.axis_size("z")
    k_rows = tokens.shape[1] // 2
    kept = lax.dynamic_slice_in_dim(tokens, k_half * k_rows, k_rows, 1)
    given = lax.dynamic_slice_in_dim(tokens, (1 - k_half) * k_rows, k_rows, 1)
    given = lax.ppermute(given, "yl", SWAP)

    up = [(i, (i + 1) % n_z) for i in range(n_z)]
    down = [(i, (i - 1) % n_z) for i in range(n_z)]
    own = jnp.zeros((n_z,) + mine.shape, bf16)

    def place(total, block, offset, row=0):
        return lax.dynamic_update_slice(total, block[None], ((z_pos + offset) % n_z, row, 0))

    own = place(own, mine, 0)
    above = below = mine
    for i in range(1, n_z // 2):
        below = lax.ppermute(below, "z", up)
        above = lax.ppermute(above, "z", down)
        own = place(place(own, below, -i), above, i)
    below = lax.ppermute(below[: rows // 2], "z", up)
    above = lax.ppermute(above[rows // 2 :], "z", down)
    own = place(place(own, below, n_z // 2), above, n_z // 2, rows // 2)
    theirs = lax.ppermute(own, "core", SWAP)

    width = out_weight.shape[1] // (n_yh * n_x)
    pieces = repack(out_weight, norm_gain, n_yh, n_x)
    group_weight = lax.all_to_all(pieces, "x", 0, 0)
    group_weight = group_weight.reshape(n_x * channels, n_yh * width)

    def by_core(values):
        split = values.reshape(tok_rows, n_z, 2, rows)
        first = split[:, :, 0].reshape(tok_rows, n_z * rows)
        second = split[:, :, 1].reshape(tok_rows, n_z * rows)
        return jnp.where(c_pos == 0, first, second), jnp.where(c_pos == 0, second, first)

    def product(pair):
        return sum(
            jnp.dot(left, right.reshape(n_z * rows, -1), preferred_element_type=f32)
            for left, right in zip(pair, (own, theirs))
        )

    kept, given = by_core(kept), by_core(given)
    away = lax.ppermute(product(given).astype(bf16), "yl", SWAP)
    acc = product(kept)
    acc = acc + away.astype(f32)
    acc, group_weight = lax.optimization_barrier((acc, group_weight))
    zx = acc[:, :zx_cols].reshape(tok_rows, heads_here, 2, head_size)
    bc_raw = acc[:, zx_cols : zx_cols + group_cols]
    dt_raw = acc[:, zx_cols + group_cols : zx_cols + group_cols + heads_here]
    gate = zx[:, :, 0, :].astype(f32).reshape(tok_rows, channels)
    xin = zx[:, :, 1, :].reshape(tok_rows, channels)
    xconv = causal(xin, conv_x, LEN)
    conv_group = lax.dynamic_slice_in_dim(conv_bc, group_id * group_cols, group_cols, 1)
    bconv = causal(bc_raw, conv_group, LEN)
    count = tok_rows // LEN
    steps = jax.nn.softplus(dt_raw.astype(f32) + dt_bias).reshape(count, LEN, heads_here)
    cum = jnp.cumsum(-steps * jnp.exp(a_log), axis=1)
    seg = cum[:, :, None, :] - cum[:, None, :, :]
    lower = jnp.arange(LEN)[:, None] >= jnp.arange(LEN)[None, :]
    decay = jnp.exp(jnp.where(lower[None, :, :, None], seg, -1e30))
    bseq = bconv[:, :state].reshape(count, LEN, state)
    cseq = bconv[:, state:].reshape(count, LEN, state)
    inner = jnp.einsum("btn,bsn->bts", cseq, bseq, preferred_element_type=f32)
    weights = inner[..., None] * decay * steps[:, None, :, :]
    xval = xconv.astype(f32).reshape(count, LEN, heads_here, head_size)
    ys = jnp.einsum("btsh,bshp->bthp", weights, xval, precision=lax.Precision.HIGHEST)
    ys = ys + d_skip[None, None, :, None] * xval
    gated = (ys.reshape(tok_rows, channels) * jax.nn.silu(gate)).astype(bf16)

    spread = jnp.broadcast_to(gated[None], (n_x, tok_rows, channels))
    group = lax.all_to_all(spread, "x", 0, 0)
    squares = jnp.sum(jnp.square(group.astype(f32)), axis=(0, 2))
    scale = lax.rsqrt(squares / (n_x * channels) + 1e-05)
    parts = jnp.einsum(
        "xtc,xcyw->ytw",
        group,
        group_weight.reshape(n_x, channels, n_yh, width),
        preferred_element_type=f32,
    )
    parts = (parts * scale[None, :, None]).astype(bf16)
    got = lax.all_to_all(parts, "yh", 0, 0)
    return jnp.sum(got.astype(f32), axis=0).astype(bf16)


def solution(mesh):
    fine = Mesh(mesh.devices.reshape(SIZES), FSDP + HEAD)
    in_specs = (
        P(FSDP, None),
        P(FSDP, HEAD, None),
        P(FSDP, HEAD),
        P(FSDP, None),
        P(None, HEAD),
        P(),
        P(HEAD),
        P(HEAD),
        P(HEAD),
        P(HEAD),
        P(HEAD, None),
    )
    return jax.shard_map(
        layer, mesh=fine, in_specs=in_specs, out_specs=P(FSDP, HEAD), check_vma=False
    )
```

```python
import jax
import jax.numpy as jnp
from jax import lax
from jax.experimental import pallas as pl
from jax.sharding import Mesh, PartitionSpec as P

LEN = 256
FSDP = ("yl", "z", "core")
HEAD = ("yh", "x")
SIZES = (2, 8, 2, 4, 8)
SWAP = [(0, 1), (1, 0)]


def repack(weight, gain, n_yh, n_x):
    rows, columns = weight.shape
    width = columns // (n_yh * n_x)

    def kernel(gain_ref, *refs):
        out_ref = refs[-1]
        for i, ref in enumerate(refs[:-1]):
            value = ref[...].astype(jnp.float32) * gain_ref[...]
            out_ref[0, :, i * width : (i + 1) * width] = value.astype(jnp.bfloat16)

    def spec(i):
        return pl.BlockSpec((rows, width), lambda x: (0, i * n_x + x))

    return pl.pallas_call(
        kernel,
        grid=(n_x,),
        in_specs=[pl.BlockSpec((rows, 1), lambda x: (0, 0))] + [spec(i) for i in range(n_yh)],
        out_specs=pl.BlockSpec((1, rows, n_yh * width), lambda x: (x, 0, 0)),
        out_shape=jax.ShapeDtypeStruct((n_x, rows, n_yh * width), jnp.bfloat16),
        cost_estimate=pl.CostEstimate(
            flops=rows * columns, bytes_accessed=4 * rows * columns, transcendentals=0
        ),
        name="repack",
    )(gain[:, None], *[weight] * n_yh)


def settle(values):
    return lax.optimization_barrier(values.astype(jnp.bfloat16))


def causal(values, kernel, seq_len):
    columns = values.shape[1]
    seqs = values.reshape(-1, seq_len, columns).astype(jnp.float32)
    taps = kernel.shape[0]
    padded = jnp.pad(seqs, ((0, 0), (taps - 1, 0), (0, 0)))
    total = jnp.zeros(seqs.shape, jnp.float32)
    for tap in range(taps):
        total = total + kernel[tap] * padded[:, tap : tap + seq_len]
    return settle(jax.nn.silu(total).reshape(-1, columns))


def layer(
    tokens,
    zx_weight,
    dt_weight,
    bc_weight,
    conv_x,
    conv_bc,
    a_log,
    dt_bias,
    d_skip,
    norm_gain,
    out_weight,
):
    f32, bf16 = jnp.float32, jnp.bfloat16
    tok_rows = tokens.shape[0]
    rows, heads_here, two_p = zx_weight.shape
    head_size = two_p // 2
    channels = heads_here * head_size
    n_yh, n_x = lax.axis_size("yh"), lax.axis_size("x")
    group_id = lax.axis_index("yh")
    group_cols = bc_weight.shape[1] // n_yh
    state = group_cols // 2
    bc_part = lax.dynamic_slice_in_dim(bc_weight, group_id * group_cols, group_cols, 1)
    zx_cols = heads_here * two_p
    pad = -(zx_cols + group_cols + heads_here) % 128
    mine = jnp.concatenate(
        [
            zx_weight.reshape(rows, zx_cols),
            bc_part,
            dt_weight,
            jnp.zeros((rows, pad), bf16),
        ],
        axis=1,
    )
    k_half = lax.axis_index("yl")
    k_rows = tokens.shape[1] // 2
    kept = lax.dynamic_slice_in_dim(tokens, k_half * k_rows, k_rows, 1)
    given = lax.dynamic_slice_in_dim(tokens, (1 - k_half) * k_rows, k_rows, 1)
    given = lax.ppermute(given, "yl", SWAP)

    whole = lax.all_gather(mine, ("z", "core"), axis=0, tiled=True)

    width = out_weight.shape[1] // (n_yh * n_x)
    pieces = repack(out_weight, norm_gain, n_yh, n_x)
    group_weight = lax.all_to_all(pieces, "x", 0, 0)
    group_weight = group_weight.reshape(n_x * channels, n_yh * width)

    away = jnp.dot(given, whole, preferred_element_type=f32)
    away = lax.ppermute(away.astype(bf16), "yl", SWAP)
    acc = jnp.dot(kept, whole, preferred_element_type=f32)
    acc = acc + away.astype(f32)
    acc, group_weight = lax.optimization_barrier((acc, group_weight))
    zx = acc[:, :zx_cols].reshape(tok_rows, heads_here, 2, head_size)
    bc_raw = acc[:, zx_cols : zx_cols + group_cols]
    dt_raw = acc[:, zx_cols + group_cols : zx_cols + group_cols + heads_here]
    gate = zx[:, :, 0, :].astype(f32).reshape(tok_rows, channels)
    xin = zx[:, :, 1, :].reshape(tok_rows, channels)
    xconv = causal(xin, conv_x, LEN)
    conv_group = lax.dynamic_slice_in_dim(conv_bc, group_id * group_cols, group_cols, 1)
    bconv = causal(bc_raw, conv_group, LEN)
    count = tok_rows // LEN
    steps = jax.nn.softplus(dt_raw.astype(f32) + dt_bias).reshape(count, LEN, heads_here)
    cum = jnp.cumsum(-steps * jnp.exp(a_log), axis=1)
    seg = cum[:, :, None, :] - cum[:, None, :, :]
    lower = jnp.arange(LEN)[:, None] >= jnp.arange(LEN)[None, :]
    decay = jnp.exp(jnp.where(lower[None, :, :, None], seg, -1e30))
    bseq = bconv[:, :state].reshape(count, LEN, state)
    cseq = bconv[:, state:].reshape(count, LEN, state)
    inner = jnp.einsum("btn,bsn->bts", cseq, bseq, preferred_element_type=f32)
    weights = inner[..., None] * decay * steps[:, None, :, :]
    xval = xconv.astype(f32).reshape(count, LEN, heads_here, head_size)
    ys = jnp.einsum("btsh,bshp->bthp", weights, xval, precision=lax.Precision.HIGHEST)
    ys = ys + d_skip[None, None, :, None] * xval
    gated = (ys.reshape(tok_rows, channels) * jax.nn.silu(gate)).astype(bf16)

    spread = jnp.broadcast_to(gated[None], (n_x, tok_rows, channels))
    group = lax.all_to_all(spread, "x", 0, 0)
    squares = jnp.sum(jnp.square(group.astype(f32)), axis=(0, 2))
    scale = lax.rsqrt(squares / (n_x * channels) + 1e-05)
    parts = jnp.einsum(
        "xtc,xcyw->ytw",
        group,
        group_weight.reshape(n_x, channels, n_yh, width),
        preferred_element_type=f32,
    )
    parts = (parts * scale[None, :, None]).astype(bf16)
    got = lax.all_to_all(parts, "yh", 0, 0)
    return jnp.sum(got.astype(f32), axis=0).astype(bf16)


def solution(mesh):
    fine = Mesh(mesh.devices.reshape(SIZES), FSDP + HEAD)
    in_specs = (
        P(FSDP, None),
        P(FSDP, HEAD, None),
        P(FSDP, HEAD),
        P(FSDP, None),
        P(None, HEAD),
        P(),
        P(HEAD),
        P(HEAD),
        P(HEAD),
        P(HEAD),
        P(HEAD, None),
    )
    return jax.shard_map(
        layer, mesh=fine, in_specs=in_specs, out_specs=P(FSDP, HEAD), check_vma=False
    )
```

```python
import jax
import jax.numpy as jnp
from jax import lax
from jax.experimental import pallas as pl
from jax.experimental.pallas import tpu as pltpu
from jax.sharding import Mesh, PartitionSpec as P

FSDP = ("yl", "z", "core")
HEAD = ("yh", "x")
SIZES = (2, 8, 2, 4, 8)
SWAP = [(0, 1), (1, 0)]


def repack(weight, gain, n_yh, n_x):
    rows, columns = weight.shape
    width = columns // (n_yh * n_x)

    step = rows // 8

    def kernel(gain_ref, weight_ref, out_ref):
        gains = gain_ref[...]
        for x in range(n_x):
            for y in range(n_yh):
                start = (y * n_x + x) * width
                value = weight_ref[:, start : start + width].astype(jnp.float32) * gains
                out_ref[x, :, y * width : (y + 1) * width] = value.astype(jnp.bfloat16)

    return pl.pallas_call(
        kernel,
        grid=(rows // step,),
        in_specs=[
            pl.BlockSpec((step, 1), lambda i: (i, 0)),
            pl.BlockSpec((step, columns), lambda i: (i, 0)),
        ],
        out_specs=pl.BlockSpec((n_x, step, n_yh * width), lambda i: (0, i, 0)),
        out_shape=jax.ShapeDtypeStruct((n_x, rows, n_yh * width), jnp.bfloat16),
        cost_estimate=pl.CostEstimate(
            flops=rows * columns, bytes_accessed=4 * rows * columns, transcendentals=0
        ),
        name="repack",
    )(gain[:, None], weight)


def silu(values):
    return values * jax.nn.sigmoid(values)


def causal(values, taps_ref, columns):
    rows = lax.broadcasted_iota(jnp.int32, values.shape, 0)
    n_taps = taps_ref.shape[0]
    total = taps_ref[n_taps - 1 : n_taps, columns] * values
    for back in range(1, n_taps):
        moved = jnp.where(rows >= back, pltpu.roll(values, back, 0), 0.0)
        total = total + taps_ref[n_taps - 1 - back : n_taps - back, columns] * moved
    return silu(total).astype(jnp.bfloat16)


def mixing_kernel(own_ref, away_ref, taps_ref, rate_ref, bias_ref, out_ref):
    f32 = jnp.float32
    heads, length, _ = out_ref.shape
    state = taps_ref.shape[1] // 2
    both = own_ref[...] + away_ref[...].astype(f32)
    keys = causal(both[:, :state], taps_ref, slice(0, state))
    queries = causal(both[:, state : 2 * state], taps_ref, slice(state, 2 * state))
    inner = lax.dot_general(queries, keys, (((1,), (1,)), ((), ())), preferred_element_type=f32)
    steps = jax.nn.softplus(both[:, 2 * state :] + bias_ref[...])
    rates = -steps * jnp.exp(rate_ref[...])
    shape = (length, length)
    lower = lax.broadcasted_iota(jnp.int32, shape, 0) >= lax.broadcasted_iota(jnp.int32, shape, 1)
    cum = jnp.dot(
        jnp.where(lower, 1.0, 0.0),
        rates,
        precision=lax.Precision.HIGHEST,
        preferred_element_type=f32,
    )
    cum_t, steps_t = cum.T, steps.T
    for h in range(heads):
        seg = cum[:, h : h + 1] - cum_t[h : h + 1, :]
        decay = jnp.exp(jnp.where(lower, seg, -1e30))
        out_ref[h] = (inner * decay * steps_t[h : h + 1, :]).astype(jnp.bfloat16)


def gated_kernel(own_ref, away_ref, taps_ref, skip_ref, mix_ref, out_ref):
    f32 = jnp.float32
    heads = mix_ref.shape[0]
    length = own_ref.shape[0]
    wide = own_ref.shape[1] // heads
    half = wide // 2
    first = lax.broadcasted_iota(jnp.int32, (length, wide), 1) < half
    kept = None
    for h in range(heads):
        columns = slice(h * wide, (h + 1) * wide)
        both = own_ref[:, columns] + away_ref[:, columns].astype(f32)
        conv = causal(both, taps_ref, columns)
        out = jnp.dot(mix_ref[h], conv, preferred_element_type=f32)
        out = out + skip_ref[:, columns] * conv.astype(f32)
        out = out * pltpu.roll(silu(both), half, 1)
        if h % 2 == 0:
            kept = pltpu.roll(out, half, 1)
        else:
            pair = jnp.where(first, kept, out).astype(jnp.bfloat16)
            for copy in range(out_ref.shape[0]):
                out_ref[copy, :, (h // 2) * wide : (h // 2 + 1) * wide] = pair


def on_chip(kernel, out_shape, flops, *args):
    moved = sum(a.size * a.dtype.itemsize for a in args) + 2 * out_shape.size
    return pl.pallas_call(
        kernel,
        out_shape=out_shape,
        cost_estimate=pl.CostEstimate(flops=flops, bytes_accessed=moved, transcendentals=0),
    )(*args)


def layer(
    tokens,
    zx_weight,
    dt_weight,
    bc_weight,
    conv_x,
    conv_bc,
    a_log,
    dt_bias,
    d_skip,
    norm_gain,
    out_weight,
):
    f32, bf16 = jnp.float32, jnp.bfloat16
    tok_rows = tokens.shape[0]
    rows, heads_here, two_p = zx_weight.shape
    head_size = two_p // 2
    channels = heads_here * head_size
    n_yh, n_x = lax.axis_size("yh"), lax.axis_size("x")
    group_id = lax.axis_index("yh")
    group_cols = bc_weight.shape[1] // n_yh
    bc_part = lax.dynamic_slice_in_dim(bc_weight, group_id * group_cols, group_cols, 1)
    zx_cols = heads_here * two_p
    pad = -(zx_cols + group_cols + heads_here) % 128
    mine = jnp.concatenate(
        [
            zx_weight.reshape(rows, zx_cols),
            bc_part,
            dt_weight,
            jnp.zeros((rows, pad), bf16),
        ],
        axis=1,
    )
    k_half = lax.axis_index("yl")
    k_rows = tokens.shape[1] // 2
    kept = lax.dynamic_slice_in_dim(tokens, k_half * k_rows, k_rows, 1)
    given = lax.dynamic_slice_in_dim(tokens, (1 - k_half) * k_rows, k_rows, 1)
    given = lax.ppermute(given, "yl", SWAP)

    whole = lax.all_gather(mine, ("z", "core"), axis=0, tiled=True)

    width = out_weight.shape[1] // (n_yh * n_x)
    pieces = repack(out_weight, norm_gain, n_yh, n_x)
    group_weight = lax.all_to_all(pieces, "x", 0, 0)
    group_weight = group_weight.reshape(n_x * channels, n_yh * width)

    def padded(values):
        return jnp.pad(values, (0, 128 - heads_here))[None]

    conv_group = lax.dynamic_slice_in_dim(conv_bc, group_id * group_cols, group_cols, 1)
    taps = conv_x.shape[0]
    x_taps = conv_x.reshape(taps, heads_here, head_size)
    x_taps = jnp.concatenate([jnp.zeros_like(x_taps), x_taps], axis=2).reshape(taps, zx_cols)
    skips = jnp.repeat(d_skip, two_p)[None]
    rate, bias = padded(a_log), padded(dt_bias)

    def product(left, columns):
        return jnp.dot(left, whole[:, columns], preferred_element_type=f32)

    small, large = slice(zx_cols, None), slice(0, zx_cols)
    small_away = lax.ppermute(product(given, small).astype(bf16), "yl", SWAP)
    large_away = lax.ppermute(product(given, large).astype(bf16), "yl", SWAP)
    small_own, large_own = product(kept, small), product(kept, large)
    mix = on_chip(
        mixing_kernel,
        jax.ShapeDtypeStruct((heads_here, tok_rows, tok_rows), bf16),
        10 * heads_here * tok_rows * tok_rows,
        small_own,
        small_away,
        conv_group,
        rate,
        bias,
    )
    mix, group_weight = lax.optimization_barrier((mix, group_weight))
    spread = on_chip(
        gated_kernel,
        jax.ShapeDtypeStruct((n_x, tok_rows, channels), bf16),
        4 * tok_rows * tok_rows * channels,
        large_own,
        large_away,
        x_taps,
        skips,
        mix,
    )
    group = lax.all_to_all(spread, "x", 0, 0)
    squares = jnp.sum(jnp.square(group.astype(f32)), axis=(0, 2))
    scale = lax.rsqrt(squares / (n_x * channels) + 1e-05)
    parts = jnp.einsum(
        "xtc,xcyw->ytw",
        group,
        group_weight.reshape(n_x, channels, n_yh, width),
        preferred_element_type=f32,
    )
    parts = (parts * scale[None, :, None]).astype(bf16)
    got = lax.all_to_all(parts, "yh", 0, 0)
    return jnp.sum(got.astype(f32), axis=0).astype(bf16)


def solution(mesh):
    fine = Mesh(mesh.devices.reshape(SIZES), FSDP + HEAD)
    in_specs = (
        P(FSDP, None),
        P(FSDP, HEAD, None),
        P(FSDP, HEAD),
        P(FSDP, None),
        P(None, HEAD),
        P(),
        P(HEAD),
        P(HEAD),
        P(HEAD),
        P(HEAD),
        P(HEAD, None),
    )
    return jax.shard_map(
        layer, mesh=fine, in_specs=in_specs, out_specs=P(FSDP, HEAD), check_vma=False
    )
```

```python
import jax
import jax.numpy as jnp
from jax import lax
from jax.experimental import pallas as pl
from jax.experimental.pallas import tpu as pltpu
from jax.sharding import Mesh, PartitionSpec as P

FSDP = ("yl", "z", "core")
HEAD = ("yh", "x")
SIZES = (2, 8, 2, 4, 8)
SWAP = [(0, 1), (1, 0)]


def repack(weight, gain, n_yh, n_x, part):
    rows = weight.shape[0]
    columns = weight.shape[1] // 2
    width = columns // (n_yh * n_x)
    step = rows // 4

    def kernel(part_ref, gain_ref, weight_ref, out_ref):
        gains = gain_ref[...]
        for x in range(n_x):
            for y in range(n_yh):
                start = (y * n_x + x) * width
                value = weight_ref[:, start : start + width].astype(jnp.float32) * gains
                out_ref[x, :, y * width : (y + 1) * width] = value.astype(jnp.bfloat16)

    return pl.pallas_call(
        kernel,
        grid_spec=pltpu.PrefetchScalarGridSpec(
            num_scalar_prefetch=1,
            grid=(rows // step,),
            in_specs=[
                pl.BlockSpec((step, 1), lambda i, part: (i, 0)),
                pl.BlockSpec((step, columns), lambda i, part: (i, part[0])),
            ],
            out_specs=pl.BlockSpec((n_x, step, n_yh * width), lambda i, part: (0, i, 0)),
        ),
        out_shape=jax.ShapeDtypeStruct((n_x, rows, n_yh * width), jnp.bfloat16),
        cost_estimate=pl.CostEstimate(
            flops=rows * columns, bytes_accessed=4 * rows * columns, transcendentals=0
        ),
        name="repack",
    )(part[None], gain[:, None], weight)


def silu(values):
    return values * jax.nn.sigmoid(values)


def causal(values, taps_ref, columns):
    rows = lax.broadcasted_iota(jnp.int32, values.shape, 0)
    n_taps = taps_ref.shape[0]
    total = taps_ref[n_taps - 1 : n_taps, columns] * values
    for back in range(1, n_taps):
        moved = jnp.where(rows >= back, pltpu.roll(values, back, 0), 0.0)
        total = total + taps_ref[n_taps - 1 - back : n_taps - back, columns] * moved
    return silu(total).astype(jnp.bfloat16)


def mixing_kernel(own_ref, away_ref, taps_ref, rate_ref, bias_ref, out_ref):
    f32 = jnp.float32
    heads, length, _ = out_ref.shape
    state = taps_ref.shape[1] // 2
    both = own_ref[...] + away_ref[...].astype(f32)
    keys = causal(both[:, :state], taps_ref, slice(0, state))
    queries = causal(both[:, state : 2 * state], taps_ref, slice(state, 2 * state))
    inner = lax.dot_general(queries, keys, (((1,), (1,)), ((), ())), preferred_element_type=f32)
    steps = jax.nn.softplus(both[:, 2 * state :] + bias_ref[...])
    rates = -steps * jnp.exp(rate_ref[...])
    shape = (length, length)
    lower = lax.broadcasted_iota(jnp.int32, shape, 0) >= lax.broadcasted_iota(jnp.int32, shape, 1)
    cum = jnp.dot(
        jnp.where(lower, 1.0, 0.0),
        rates,
        precision=lax.Precision.HIGHEST,
        preferred_element_type=f32,
    )
    cum_t, steps_t = cum.T, steps.T
    for h in range(heads):
        seg = cum[:, h : h + 1] - cum_t[h : h + 1, :]
        decay = jnp.exp(jnp.where(lower, seg, -1e30))
        out_ref[h] = (inner * decay * steps_t[h : h + 1, :]).astype(jnp.bfloat16)


def gated_kernel(own_ref, away_ref, taps_ref, skip_ref, mix_ref, out_ref):
    f32 = jnp.float32
    heads = mix_ref.shape[0]
    length = own_ref.shape[0]
    wide = own_ref.shape[1] // heads
    half = wide // 2
    first = lax.broadcasted_iota(jnp.int32, (length, wide), 1) < half
    kept = None
    for h in range(heads):
        columns = slice(h * wide, (h + 1) * wide)
        both = own_ref[:, columns] + away_ref[:, columns].astype(f32)
        conv = causal(both, taps_ref, columns)
        out = jnp.dot(mix_ref[h], conv, preferred_element_type=f32)
        out = out + skip_ref[:, columns] * conv.astype(f32)
        out = out * pltpu.roll(silu(both), half, 1)
        if h % 2 == 0:
            kept = pltpu.roll(out, half, 1)
        else:
            pair = jnp.where(first, kept, out).astype(jnp.bfloat16)
            for copy in range(out_ref.shape[0]):
                out_ref[copy, :, (h // 2) * wide : (h // 2 + 1) * wide] = pair


def on_chip(kernel, out_shape, flops, *args):
    moved = sum(a.size * a.dtype.itemsize for a in args) + 2 * out_shape.size
    return pl.pallas_call(
        kernel,
        out_shape=out_shape,
        cost_estimate=pl.CostEstimate(flops=flops, bytes_accessed=moved, transcendentals=0),
    )(*args)


def layer(
    tokens,
    zx_weight,
    dt_weight,
    bc_weight,
    conv_x,
    conv_bc,
    a_log,
    dt_bias,
    d_skip,
    norm_gain,
    out_weight,
):
    f32, bf16 = jnp.float32, jnp.bfloat16
    tok_rows = tokens.shape[0]
    rows, heads_here, two_p = zx_weight.shape
    head_size = two_p // 2
    channels = heads_here * head_size
    n_yh, n_x = lax.axis_size("yh"), lax.axis_size("x")
    group_id = lax.axis_index("yh")
    group_cols = bc_weight.shape[1] // n_yh
    bc_part = lax.dynamic_slice_in_dim(bc_weight, group_id * group_cols, group_cols, 1)
    zx_cols = heads_here * two_p
    pad = -(zx_cols + group_cols + heads_here) % 128
    mine = jnp.concatenate(
        [
            zx_weight.reshape(rows, zx_cols),
            bc_part,
            dt_weight,
            jnp.zeros((rows, pad), bf16),
        ],
        axis=1,
    )
    k_half = lax.axis_index("yl")
    k_rows = tokens.shape[1] // 2
    kept = lax.dynamic_slice_in_dim(tokens, k_half * k_rows, k_rows, 1)
    given = lax.dynamic_slice_in_dim(tokens, (1 - k_half) * k_rows, k_rows, 1)
    given = lax.ppermute(given, "yl", SWAP)

    n_z, core = lax.axis_size("z"), lax.axis_index("core")
    copies = jnp.broadcast_to(mine[None], (n_z,) + mine.shape)
    own = lax.all_to_all(copies, "z", 0, 0).reshape(n_z * rows, -1)
    width = out_weight.shape[1] // (n_yh * n_x)
    pieces = repack(out_weight, norm_gain, n_yh // 2, n_x, core)
    half_own = lax.all_to_all(pieces, "x", 0, 0)

    def by_core(values):
        split = values.reshape(tok_rows, n_z, 2, rows)
        first = split[:, :, 0].reshape(tok_rows, n_z * rows)
        second = split[:, :, 1].reshape(tok_rows, n_z * rows)
        return jnp.where(core == 0, first, second), jnp.where(core == 0, second, first)

    kept, given = by_core(kept), by_core(given)

    def padded(values):
        return jnp.pad(values, (0, 128 - heads_here))[None]

    conv_group = lax.dynamic_slice_in_dim(conv_bc, group_id * group_cols, group_cols, 1)
    taps = conv_x.shape[0]
    x_taps = conv_x.reshape(taps, heads_here, head_size)
    x_taps = jnp.concatenate([jnp.zeros_like(x_taps), x_taps], axis=2).reshape(taps, zx_cols)
    skips = jnp.repeat(d_skip, two_p)[None]
    rate, bias = padded(a_log), padded(dt_bias)

    ready = (own, kept, given, conv_group, x_taps, skips, rate, bias)
    own, kept, given, conv_group, x_taps, skips, rate, bias = lax.optimization_barrier(ready)
    theirs = lax.ppermute(own, "core", SWAP)
    small, large = slice(zx_cols, None), slice(0, zx_cols)

    def product(left, columns, begun):
        return begun[:, columns] + jnp.dot(
            left, theirs[:, columns], preferred_element_type=f32
        )

    given_begun = jnp.dot(given[0], own, preferred_element_type=f32)
    kept_begun = jnp.dot(kept[0], own, preferred_element_type=f32)
    small_away = product(given[1], small, given_begun).astype(bf16)
    small_away = lax.ppermute(small_away, "yl", SWAP)
    large_away = product(given[1], large, given_begun).astype(bf16)
    large_away = lax.ppermute(large_away, "yl", SWAP)
    small_own = product(kept[1], small, kept_begun)
    large_own = product(kept[1], large, kept_begun)
    mix = on_chip(
        mixing_kernel,
        jax.ShapeDtypeStruct((heads_here, tok_rows, tok_rows), bf16),
        10 * heads_here * tok_rows * tok_rows,
        small_own,
        small_away,
        conv_group,
        rate,
        bias,
    )
    mix, half_own = lax.optimization_barrier((mix, half_own))
    half_theirs = lax.ppermute(half_own, "core", SWAP)
    spread = on_chip(
        gated_kernel,
        jax.ShapeDtypeStruct((n_x, tok_rows, channels), bf16),
        4 * tok_rows * tok_rows * channels,
        large_own,
        large_away,
        x_taps,
        skips,
        mix,
    )
    group = lax.all_to_all(spread, "x", 0, 0)
    squares = jnp.sum(jnp.square(group.astype(f32)), axis=(0, 2))
    scale = lax.rsqrt(squares / (n_x * channels) + 1e-05)

    def partial_out(half):
        half = half.reshape(n_x, channels, n_yh // 2, width)
        out = jnp.einsum("xtc,xcyw->ytw", group, half, preferred_element_type=f32)
        return (out * scale[None, :, None]).astype(bf16)

    ours, others = partial_out(half_own), partial_out(half_theirs)
    parts = jnp.concatenate(
        [jnp.where(core == 0, ours, others), jnp.where(core == 0, others, ours)], axis=0
    )
    got = lax.all_to_all(parts, "yh", 0, 0)
    return jnp.sum(got.astype(f32), axis=0).astype(bf16)


def solution(mesh):
    fine = Mesh(mesh.devices.reshape(SIZES), FSDP + HEAD)
    in_specs = (
        P(FSDP, None),
        P(FSDP, HEAD, None),
        P(FSDP, HEAD),
        P(FSDP, None),
        P(None, HEAD),
        P(),
        P(HEAD),
        P(HEAD),
        P(HEAD),
        P(HEAD),
        P(HEAD, None),
    )
    return jax.shard_map(
        layer, mesh=fine, in_specs=in_specs, out_specs=P(FSDP, HEAD), check_vma=False
    )
```

```python
import jax
import jax.numpy as jnp
from jax import lax
from jax.experimental import pallas as pl
from jax.experimental.pallas import tpu as pltpu
from jax.sharding import Mesh, PartitionSpec as P

FSDP = ("yl", "z", "core")
HEAD = ("yh", "x")
SIZES = (2, 8, 2, 4, 8)
SWAP = [(0, 1), (1, 0)]


def repack(weight, gain, n_yh, n_x, part):
    rows = weight.shape[0]
    columns = weight.shape[1] // 2
    width = columns // (n_yh * n_x)
    step = rows // 4

    def kernel(part_ref, gain_ref, weight_ref, out_ref):
        gains = gain_ref[...]
        for x in range(n_x):
            for y in range(n_yh):
                start = (y * n_x + x) * width
                value = weight_ref[:, start : start + width].astype(jnp.float32) * gains
                out_ref[x, :, y * width : (y + 1) * width] = value.astype(jnp.bfloat16)

    return pl.pallas_call(
        kernel,
        grid_spec=pltpu.PrefetchScalarGridSpec(
            num_scalar_prefetch=1,
            grid=(rows // step,),
            in_specs=[
                pl.BlockSpec((step, 1), lambda i, part: (i, 0)),
                pl.BlockSpec((step, columns), lambda i, part: (i, part[0])),
            ],
            out_specs=pl.BlockSpec((n_x, step, n_yh * width), lambda i, part: (0, i, 0)),
        ),
        out_shape=jax.ShapeDtypeStruct((n_x, rows, n_yh * width), jnp.bfloat16),
        cost_estimate=pl.CostEstimate(
            flops=rows * columns, bytes_accessed=4 * rows * columns, transcendentals=0
        ),
        name="repack",
    )(part[None], gain[:, None], weight)


def silu(values):
    return values * jax.nn.sigmoid(values)


def causal(values, taps_ref, columns):
    rows = lax.broadcasted_iota(jnp.int32, values.shape, 0)
    n_taps = taps_ref.shape[0]
    total = taps_ref[n_taps - 1 : n_taps, columns] * values
    for back in range(1, n_taps):
        moved = jnp.where(rows >= back, pltpu.roll(values, back, 0), 0.0)
        total = total + taps_ref[n_taps - 1 - back : n_taps - back, columns] * moved
    return silu(total).astype(jnp.bfloat16)


def mixing_kernel(own_ref, away_ref, taps_ref, rate_ref, bias_ref, out_ref):
    f32 = jnp.float32
    heads, length, _ = out_ref.shape
    state = taps_ref.shape[1] // 2
    both = own_ref[...] + away_ref[...].astype(f32)
    keys = causal(both[:, :state], taps_ref, slice(0, state))
    queries = causal(both[:, state : 2 * state], taps_ref, slice(state, 2 * state))
    inner = lax.dot_general(queries, keys, (((1,), (1,)), ((), ())), preferred_element_type=f32)
    steps = jax.nn.softplus(both[:, 2 * state :] + bias_ref[...])
    rates = -steps * jnp.exp(rate_ref[...])
    shape = (length, length)
    lower = lax.broadcasted_iota(jnp.int32, shape, 0) >= lax.broadcasted_iota(jnp.int32, shape, 1)
    cum = jnp.dot(
        jnp.where(lower, 1.0, 0.0),
        rates,
        precision=lax.Precision.HIGHEST,
        preferred_element_type=f32,
    )
    cum_t, steps_t = cum.T, steps.T
    for h in range(heads):
        seg = cum[:, h : h + 1] - cum_t[h : h + 1, :]
        decay = jnp.exp(jnp.where(lower, seg, -1e30))
        out_ref[h] = (inner * decay * steps_t[h : h + 1, :]).astype(jnp.bfloat16)


def gated_kernel(own_ref, away_ref, taps_ref, skip_ref, mix_ref, out_ref):
    f32 = jnp.float32
    heads = mix_ref.shape[0]
    length = own_ref.shape[0]
    wide = own_ref.shape[1] // heads
    half = wide // 2
    first = lax.broadcasted_iota(jnp.int32, (length, wide), 1) < half
    kept = None
    for h in range(heads):
        columns = slice(h * wide, (h + 1) * wide)
        both = own_ref[:, columns] + away_ref[:, columns].astype(f32)
        conv = causal(both, taps_ref, columns)
        out = jnp.dot(mix_ref[h], conv, preferred_element_type=f32)
        out = out + skip_ref[:, columns] * conv.astype(f32)
        out = out * pltpu.roll(silu(both), half, 1)
        if h % 2 == 0:
            kept = pltpu.roll(out, half, 1)
        else:
            pair = jnp.where(first, kept, out).astype(jnp.bfloat16)
            for copy in range(out_ref.shape[0]):
                out_ref[copy, :, (h // 2) * wide : (h // 2 + 1) * wide] = pair


def finish_kernel(core_ref, group_ref, own_ref, theirs_ref, out_ref):
    f32 = jnp.float32
    n_x, rows, channels = group_ref.shape
    width = out_ref.shape[2]
    many = own_ref.shape[2] // width
    squares = jnp.zeros((rows, 1), f32)
    totals = [jnp.zeros((rows, many * width), f32) for _ in range(2)]
    for x in range(n_x):
        values = group_ref[x]
        squares += jnp.sum(jnp.square(values.astype(f32)), axis=1, keepdims=True)
        totals = [
            total + jnp.dot(values, ref[x], preferred_element_type=f32)
            for total, ref in zip(totals, (own_ref, theirs_ref))
        ]
    scale = lax.rsqrt(squares / (n_x * channels) + 1e-05)
    start = core_ref[0] * many
    for total, first in zip(totals, (start, many - start)):
        done = (total * scale).astype(jnp.bfloat16)
        for y in range(many):
            out_ref[first + y] = done[:, y * width : (y + 1) * width]


def on_chip(kernel, out_shape, flops, *args):
    moved = sum(a.size * a.dtype.itemsize for a in args) + 2 * out_shape.size
    return pl.pallas_call(
        kernel,
        out_shape=out_shape,
        cost_estimate=pl.CostEstimate(flops=flops, bytes_accessed=moved, transcendentals=0),
    )(*args)


def layer(
    tokens,
    zx_weight,
    dt_weight,
    bc_weight,
    conv_x,
    conv_bc,
    a_log,
    dt_bias,
    d_skip,
    norm_gain,
    out_weight,
):
    f32, bf16 = jnp.float32, jnp.bfloat16
    tok_rows = tokens.shape[0]
    rows, heads_here, two_p = zx_weight.shape
    head_size = two_p // 2
    channels = heads_here * head_size
    n_yh, n_x = lax.axis_size("yh"), lax.axis_size("x")
    group_id = lax.axis_index("yh")
    group_cols = bc_weight.shape[1] // n_yh
    bc_part = lax.dynamic_slice_in_dim(bc_weight, group_id * group_cols, group_cols, 1)
    zx_cols = heads_here * two_p
    pad = -(zx_cols + group_cols + heads_here) % 128
    mine = jnp.concatenate(
        [
            zx_weight.reshape(rows, zx_cols),
            bc_part,
            dt_weight,
            jnp.zeros((rows, pad), bf16),
        ],
        axis=1,
    )
    k_half = lax.axis_index("yl")
    k_rows = tokens.shape[1] // 2
    kept = lax.dynamic_slice_in_dim(tokens, k_half * k_rows, k_rows, 1)
    given = lax.dynamic_slice_in_dim(tokens, (1 - k_half) * k_rows, k_rows, 1)
    given = lax.ppermute(given, "yl", SWAP)

    n_z, core = lax.axis_size("z"), lax.axis_index("core")
    copies = jnp.broadcast_to(mine[None], (n_z,) + mine.shape)
    own = lax.all_to_all(copies, "z", 0, 0).reshape(n_z * rows, -1)
    width = out_weight.shape[1] // (n_yh * n_x)
    pieces = repack(out_weight, norm_gain, n_yh // 2, n_x, core)
    x_pos = lax.axis_index("x")

    def piece(k):
        return lax.dynamic_slice_in_dim(pieces, (x_pos + k) % n_x, 1, 0)

    half_own = jnp.zeros_like(pieces)
    half_own = lax.dynamic_update_slice_in_dim(half_own, piece(0), x_pos, 0)
    for k in range(1, n_x):
        came = lax.ppermute(piece(k), "x", [(i, (i + k) % n_x) for i in range(n_x)])
        half_own = lax.dynamic_update_slice_in_dim(half_own, came, (x_pos - k) % n_x, 0)

    def by_core(values):
        split = values.reshape(tok_rows, n_z, 2, rows)
        first = split[:, :, 0].reshape(tok_rows, n_z * rows)
        second = split[:, :, 1].reshape(tok_rows, n_z * rows)
        return jnp.where(core == 0, first, second), jnp.where(core == 0, second, first)

    kept, given = by_core(kept), by_core(given)

    def padded(values):
        return jnp.pad(values, (0, 128 - heads_here))[None]

    conv_group = lax.dynamic_slice_in_dim(conv_bc, group_id * group_cols, group_cols, 1)
    taps = conv_x.shape[0]
    x_taps = conv_x.reshape(taps, heads_here, head_size)
    x_taps = jnp.concatenate([jnp.zeros_like(x_taps), x_taps], axis=2).reshape(taps, zx_cols)
    skips = jnp.repeat(d_skip, two_p)[None]
    rate, bias = padded(a_log), padded(dt_bias)

    ready = (own, kept, given, conv_group, x_taps, skips, rate, bias, half_own)
    ready = lax.optimization_barrier(ready)
    own, kept, given, conv_group, x_taps, skips, rate, bias, half_own = ready
    theirs = lax.ppermute(own, "core", SWAP)
    small, large = slice(zx_cols, None), slice(0, zx_cols)

    def product(left, columns, begun):
        return begun[:, columns] + jnp.dot(
            left, theirs[:, columns], preferred_element_type=f32
        )

    given_begun = jnp.dot(given[0], own, preferred_element_type=f32)
    kept_begun = jnp.dot(kept[0], own, preferred_element_type=f32)
    small_away = product(given[1], small, given_begun).astype(bf16)
    small_away = lax.ppermute(small_away, "yl", SWAP)
    large_away = product(given[1], large, given_begun).astype(bf16)
    large_away = lax.ppermute(large_away, "yl", SWAP)
    small_own = product(kept[1], small, kept_begun)
    large_own = product(kept[1], large, kept_begun)
    mix = on_chip(
        mixing_kernel,
        jax.ShapeDtypeStruct((heads_here, tok_rows, tok_rows), bf16),
        10 * heads_here * tok_rows * tok_rows,
        small_own,
        small_away,
        conv_group,
        rate,
        bias,
    )
    half_theirs = lax.ppermute(half_own, "core", SWAP)
    spread = on_chip(
        gated_kernel,
        jax.ShapeDtypeStruct((n_x, tok_rows, channels), bf16),
        4 * tok_rows * tok_rows * channels,
        large_own,
        large_away,
        x_taps,
        skips,
        mix,
    )
    group = lax.all_to_all(spread, "x", 0, 0)
    parts = pl.pallas_call(
        finish_kernel,
        in_specs=[pl.BlockSpec(memory_space=pltpu.SMEM)]
        + [pl.BlockSpec(memory_space=pltpu.VMEM)] * 3,
        out_shape=jax.ShapeDtypeStruct((n_yh, tok_rows, width), bf16),
        cost_estimate=pl.CostEstimate(
            flops=2 * tok_rows * n_x * channels * n_yh * width,
            bytes_accessed=6 * n_x * tok_rows * channels,
            transcendentals=0,
        ),
        name="finish",
    )(core[None], group, half_own, half_theirs)
    got = lax.all_to_all(parts, "yh", 0, 0)
    return jnp.sum(got.astype(f32), axis=0).astype(bf16)


def solution(mesh):
    fine = Mesh(mesh.devices.reshape(SIZES), FSDP + HEAD)
    in_specs = (
        P(FSDP, None),
        P(FSDP, HEAD, None),
        P(FSDP, HEAD),
        P(FSDP, None),
        P(None, HEAD),
        P(),
        P(HEAD),
        P(HEAD),
        P(HEAD),
        P(HEAD),
        P(HEAD, None),
    )
    return jax.shard_map(
        layer, mesh=fine, in_specs=in_specs, out_specs=P(FSDP, HEAD), check_vma=False
    )
```

```python
import jax
import jax.numpy as jnp
from jax import lax
from jax.experimental import pallas as pl
from jax.experimental.pallas import tpu as pltpu
from jax.sharding import Mesh, PartitionSpec as P

FSDP = ("yl", "z", "core")
HEAD = ("yh", "x")
SIZES = (2, 8, 2, 4, 8)
SWAP = [(0, 1), (1, 0)]


def repack(weight, gain, n_yh, n_x, part):
    rows = weight.shape[0]
    columns = weight.shape[1] // 2
    width = columns // (n_yh * n_x)
    step = rows // 4

    def kernel(part_ref, gain_ref, weight_ref, out_ref):
        gains = gain_ref[...]
        for x in range(n_x):
            for y in range(n_yh):
                start = (y * n_x + x) * width
                value = weight_ref[:, start : start + width].astype(jnp.float32) * gains
                out_ref[x, :, y * width : (y + 1) * width] = value.astype(jnp.bfloat16)

    return pl.pallas_call(
        kernel,
        grid_spec=pltpu.PrefetchScalarGridSpec(
            num_scalar_prefetch=1,
            grid=(rows // step,),
            in_specs=[
                pl.BlockSpec((step, 1), lambda i, part: (i, 0)),
                pl.BlockSpec((step, columns), lambda i, part: (i, part[0])),
            ],
            out_specs=pl.BlockSpec((n_x, step, n_yh * width), lambda i, part: (0, i, 0)),
        ),
        out_shape=jax.ShapeDtypeStruct((n_x, rows, n_yh * width), jnp.bfloat16),
        cost_estimate=pl.CostEstimate(
            flops=rows * columns, bytes_accessed=4 * rows * columns, transcendentals=0
        ),
        name="repack",
    )(part[None], gain[:, None], weight)


def sort_tokens(tokens, k_half, core, width):
    length, columns = tokens.shape
    step, half = length // 4, columns // 2
    blocks = half // (2 * width)

    def kernel(where_ref, near_ref, far_ref, *out_refs):
        swapped = where_ref[1] == 1
        for in_ref, out_ref in zip((near_ref, far_ref), out_refs):
            for block in range(blocks):
                first = in_ref[:, 2 * block * width : (2 * block + 1) * width]
                second = in_ref[:, (2 * block + 1) * width : (2 * block + 2) * width]
                to = slice(block * width, (block + 1) * width)
                out_ref[0, :, to] = jnp.where(swapped, second, first)
                out_ref[1, :, to] = jnp.where(swapped, first, second)

    shape = jax.ShapeDtypeStruct((2, length, half // 2), tokens.dtype)
    out_spec = pl.BlockSpec((2, step, half // 2), lambda i, where: (0, i, 0))
    return pl.pallas_call(
        kernel,
        grid_spec=pltpu.PrefetchScalarGridSpec(
            num_scalar_prefetch=1,
            grid=(length // step,),
            in_specs=[
                pl.BlockSpec((step, half), lambda i, where: (i, where[0])),
                pl.BlockSpec((step, half), lambda i, where: (i, 1 - where[0])),
            ],
            out_specs=[out_spec, out_spec],
        ),
        out_shape=[shape, shape],
        cost_estimate=pl.CostEstimate(
            flops=length * columns, bytes_accessed=4 * length * columns, transcendentals=0
        ),
        name="sort_tokens",
    )(jnp.stack([k_half, core]), tokens, tokens)


def silu(values):
    return values * jax.nn.sigmoid(values)


def causal(values, taps_ref, columns):
    rows = lax.broadcasted_iota(jnp.int32, values.shape, 0)
    n_taps = taps_ref.shape[0]
    total = taps_ref[n_taps - 1 : n_taps, columns] * values
    for back in range(1, n_taps):
        moved = jnp.where(rows >= back, pltpu.roll(values, back, 0), 0.0)
        total = total + taps_ref[n_taps - 1 - back : n_taps - back, columns] * moved
    return silu(total).astype(jnp.bfloat16)


def mixing_kernel(own_ref, away_ref, taps_ref, rate_ref, bias_ref, out_ref):
    f32 = jnp.float32
    heads, length, _ = out_ref.shape
    state = taps_ref.shape[1] // 2
    both = own_ref[...] + away_ref[...].astype(f32)
    keys = causal(both[:, :state], taps_ref, slice(0, state))
    queries = causal(both[:, state : 2 * state], taps_ref, slice(state, 2 * state))
    inner = lax.dot_general(queries, keys, (((1,), (1,)), ((), ())), preferred_element_type=f32)
    steps = jax.nn.softplus(both[:, 2 * state :] + bias_ref[...])
    rates = -steps * jnp.exp(rate_ref[...])
    shape = (length, length)
    lower = lax.broadcasted_iota(jnp.int32, shape, 0) >= lax.broadcasted_iota(jnp.int32, shape, 1)
    cum = jnp.dot(
        jnp.where(lower, 1.0, 0.0),
        rates,
        precision=lax.Precision.HIGHEST,
        preferred_element_type=f32,
    )
    cum_t, steps_t = cum.T, steps.T
    for h in range(heads):
        seg = cum[:, h : h + 1] - cum_t[h : h + 1, :]
        decay = jnp.exp(jnp.where(lower, seg, -1e30))
        out_ref[h] = (inner * decay * steps_t[h : h + 1, :]).astype(jnp.bfloat16)


def gated_kernel(own_ref, away_ref, taps_ref, skip_ref, mix_ref, out_ref):
    f32 = jnp.float32
    heads = mix_ref.shape[0]
    length = own_ref.shape[0]
    wide = own_ref.shape[1] // heads
    half = wide // 2
    first = lax.broadcasted_iota(jnp.int32, (length, wide), 1) < half
    kept = None
    for h in range(heads):
        columns = slice(h * wide, (h + 1) * wide)
        both = own_ref[:, columns] + away_ref[:, columns].astype(f32)
        conv = causal(both, taps_ref, columns)
        out = jnp.dot(mix_ref[h], conv, preferred_element_type=f32)
        out = out + skip_ref[:, columns] * conv.astype(f32)
        out = out * pltpu.roll(silu(both), half, 1)
        if h % 2 == 0:
            kept = pltpu.roll(out, half, 1)
        else:
            pair = jnp.where(first, kept, out).astype(jnp.bfloat16)
            for copy in range(out_ref.shape[0]):
                out_ref[copy, :, (h // 2) * wide : (h // 2 + 1) * wide] = pair


def finish_kernel(core_ref, group_ref, own_ref, theirs_ref, out_ref):
    f32 = jnp.float32
    n_x, rows, channels = group_ref.shape
    width = out_ref.shape[2]
    many = own_ref.shape[2] // width
    squares = jnp.zeros((rows, 1), f32)
    totals = [jnp.zeros((rows, many * width), f32) for _ in range(2)]
    for x in range(n_x):
        values = group_ref[x]
        squares += jnp.sum(jnp.square(values.astype(f32)), axis=1, keepdims=True)
        totals = [
            total + jnp.dot(values, ref[x], preferred_element_type=f32)
            for total, ref in zip(totals, (own_ref, theirs_ref))
        ]
    scale = lax.rsqrt(squares / (n_x * channels) + 1e-05)
    start = core_ref[0] * many
    for total, first in zip(totals, (start, many - start)):
        done = (total * scale).astype(jnp.bfloat16)
        for y in range(many):
            out_ref[first + y] = done[:, y * width : (y + 1) * width]


def on_chip(kernel, out_shape, flops, *args):
    moved = sum(a.size * a.dtype.itemsize for a in args) + 2 * out_shape.size
    return pl.pallas_call(
        kernel,
        out_shape=out_shape,
        cost_estimate=pl.CostEstimate(flops=flops, bytes_accessed=moved, transcendentals=0),
    )(*args)


def layer(
    tokens,
    zx_weight,
    dt_weight,
    bc_weight,
    conv_x,
    conv_bc,
    a_log,
    dt_bias,
    d_skip,
    norm_gain,
    out_weight,
):
    f32, bf16 = jnp.float32, jnp.bfloat16
    tok_rows = tokens.shape[0]
    rows, heads_here, two_p = zx_weight.shape
    head_size = two_p // 2
    channels = heads_here * head_size
    n_yh, n_x = lax.axis_size("yh"), lax.axis_size("x")
    group_id = lax.axis_index("yh")
    group_cols = bc_weight.shape[1] // n_yh
    bc_part = lax.dynamic_slice_in_dim(bc_weight, group_id * group_cols, group_cols, 1)
    zx_cols = heads_here * two_p
    pad = -(zx_cols + group_cols + heads_here) % 128
    mine = jnp.concatenate(
        [
            zx_weight.reshape(rows, zx_cols),
            bc_part,
            dt_weight,
            jnp.zeros((rows, pad), bf16),
        ],
        axis=1,
    )
    core, z_pos, n_z = lax.axis_index("core"), lax.axis_index("z"), lax.axis_size("z")
    kept, given = sort_tokens(tokens, lax.axis_index("yl"), core, rows)
    given = lax.ppermute(given, "yl", SWAP)

    up = [(i, (i + 1) % n_z) for i in range(n_z)]
    down = [(i, (i - 1) % n_z) for i in range(n_z)]
    own = jnp.zeros((n_z,) + mine.shape, bf16)

    def place(total, block, offset, row=0):
        return lax.dynamic_update_slice(total, block[None], ((z_pos + offset) % n_z, row, 0))

    own = place(own, mine, 0)
    above = below = mine
    for i in range(1, n_z // 2):
        below = lax.ppermute(below, "z", up)
        above = lax.ppermute(above, "z", down)
        own = place(place(own, below, -i), above, i)
    below = lax.ppermute(below[: rows // 2], "z", up)
    above = lax.ppermute(above[rows // 2 :], "z", down)
    own = place(place(own, below, n_z // 2), above, n_z // 2, rows // 2)
    own = own.reshape(n_z * rows, -1)

    width = out_weight.shape[1] // (n_yh * n_x)
    pieces = repack(out_weight, norm_gain, n_yh // 2, n_x, core)
    half_own = lax.all_to_all(pieces, "x", 0, 0)

    def padded(values):
        return jnp.pad(values, (0, 128 - heads_here))[None]

    conv_group = lax.dynamic_slice_in_dim(conv_bc, group_id * group_cols, group_cols, 1)
    taps = conv_x.shape[0]
    x_taps = conv_x.reshape(taps, heads_here, head_size)
    x_taps = jnp.concatenate([jnp.zeros_like(x_taps), x_taps], axis=2).reshape(taps, zx_cols)
    skips = jnp.repeat(d_skip, two_p)[None]
    rate, bias = padded(a_log), padded(dt_bias)

    theirs = lax.ppermute(own, "core", SWAP)
    small, large = slice(zx_cols, None), slice(0, zx_cols)

    def product(left, columns, begun):
        return begun[:, columns] + jnp.dot(
            left, theirs[:, columns], preferred_element_type=f32
        )

    given_begun = jnp.dot(given[0], own, preferred_element_type=f32)
    kept_begun = jnp.dot(kept[0], own, preferred_element_type=f32)
    small_away = product(given[1], small, given_begun).astype(bf16)
    small_away = lax.ppermute(small_away, "yl", SWAP)
    large_away = product(given[1], large, given_begun).astype(bf16)
    large_away = lax.ppermute(large_away, "yl", SWAP)
    small_own = product(kept[1], small, kept_begun)
    large_own = product(kept[1], large, kept_begun)
    mix = on_chip(
        mixing_kernel,
        jax.ShapeDtypeStruct((heads_here, tok_rows, tok_rows), bf16),
        10 * heads_here * tok_rows * tok_rows,
        small_own,
        small_away,
        conv_group,
        rate,
        bias,
    )
    mix, half_own = lax.optimization_barrier((mix, half_own))
    half_theirs = lax.ppermute(half_own, "core", SWAP)
    spread = on_chip(
        gated_kernel,
        jax.ShapeDtypeStruct((n_x, tok_rows, channels), bf16),
        4 * tok_rows * tok_rows * channels,
        large_own,
        large_away,
        x_taps,
        skips,
        mix,
    )
    group = lax.all_to_all(spread, "x", 0, 0)
    parts = pl.pallas_call(
        finish_kernel,
        in_specs=[pl.BlockSpec(memory_space=pltpu.SMEM)]
        + [pl.BlockSpec(memory_space=pltpu.VMEM)] * 3,
        out_shape=jax.ShapeDtypeStruct((n_yh, tok_rows, width), bf16),
        cost_estimate=pl.CostEstimate(
            flops=2 * tok_rows * n_x * channels * n_yh * width,
            bytes_accessed=6 * n_x * tok_rows * channels,
            transcendentals=0,
        ),
        name="finish",
    )(core[None], group, half_own, half_theirs)
    got = lax.all_to_all(parts, "yh", 0, 0)
    return jnp.sum(got.astype(f32), axis=0).astype(bf16)


def solution(mesh):
    fine = Mesh(mesh.devices.reshape(SIZES), FSDP + HEAD)
    in_specs = (
        P(FSDP, None),
        P(FSDP, HEAD, None),
        P(FSDP, HEAD),
        P(FSDP, None),
        P(None, HEAD),
        P(),
        P(HEAD),
        P(HEAD),
        P(HEAD),
        P(HEAD),
        P(HEAD, None),
    )
    return jax.shard_map(
        layer, mesh=fine, in_specs=in_specs, out_specs=P(FSDP, HEAD), check_vma=False
    )
```

```python
import jax
import jax.numpy as jnp
from jax import lax
from jax.experimental import pallas as pl
from jax.experimental.pallas import tpu as pltpu
from jax.sharding import Mesh, PartitionSpec as P

FSDP = ("yl", "z", "core")
HEAD = ("yh", "x")
SIZES = (2, 8, 2, 4, 8)
SWAP = [(0, 1), (1, 0)]


def repack(weight, gain, n_yh, n_x):
    rows, columns = weight.shape
    width = columns // (n_yh * n_x)

    step = rows // 8

    def kernel(gain_ref, weight_ref, out_ref):
        gains = gain_ref[...]
        for x in range(n_x):
            for y in range(n_yh):
                start = (y * n_x + x) * width
                value = weight_ref[:, start : start + width].astype(jnp.float32) * gains
                out_ref[x, :, y * width : (y + 1) * width] = value.astype(jnp.bfloat16)

    return pl.pallas_call(
        kernel,
        grid=(rows // step,),
        in_specs=[
            pl.BlockSpec((step, 1), lambda i: (i, 0)),
            pl.BlockSpec((step, columns), lambda i: (i, 0)),
        ],
        out_specs=pl.BlockSpec((n_x, step, n_yh * width), lambda i: (0, i, 0)),
        out_shape=jax.ShapeDtypeStruct((n_x, rows, n_yh * width), jnp.bfloat16),
        cost_estimate=pl.CostEstimate(
            flops=rows * columns, bytes_accessed=4 * rows * columns, transcendentals=0
        ),
        name="repack",
    )(gain[:, None], weight)


def silu(values):
    return values * jax.nn.sigmoid(values)


def causal(values, taps_ref, columns):
    rows = lax.broadcasted_iota(jnp.int32, values.shape, 0)
    n_taps = taps_ref.shape[0]
    total = taps_ref[n_taps - 1 : n_taps, columns] * values
    for back in range(1, n_taps):
        moved = jnp.where(rows >= back, pltpu.roll(values, back, 0), 0.0)
        total = total + taps_ref[n_taps - 1 - back : n_taps - back, columns] * moved
    return silu(total).astype(jnp.bfloat16)


def mixing_kernel(own_ref, away_ref, taps_ref, rate_ref, bias_ref, out_ref):
    f32 = jnp.float32
    heads, length, _ = out_ref.shape
    state = taps_ref.shape[1] // 2
    both = own_ref[...] + away_ref[...].astype(f32)
    keys = causal(both[:, :state], taps_ref, slice(0, state))
    queries = causal(both[:, state : 2 * state], taps_ref, slice(state, 2 * state))
    inner = lax.dot_general(queries, keys, (((1,), (1,)), ((), ())), preferred_element_type=f32)
    steps = jax.nn.softplus(both[:, 2 * state :] + bias_ref[...])
    rates = -steps * jnp.exp(rate_ref[...])
    shape = (length, length)
    lower = lax.broadcasted_iota(jnp.int32, shape, 0) >= lax.broadcasted_iota(jnp.int32, shape, 1)
    cum = jnp.dot(
        jnp.where(lower, 1.0, 0.0),
        rates,
        precision=lax.Precision.HIGHEST,
        preferred_element_type=f32,
    )
    cum_t, steps_t = cum.T, steps.T
    for h in range(heads):
        seg = cum[:, h : h + 1] - cum_t[h : h + 1, :]
        decay = jnp.exp(jnp.where(lower, seg, -1e30))
        out_ref[h] = (inner * decay * steps_t[h : h + 1, :]).astype(jnp.bfloat16)


def gated_kernel(own_ref, away_ref, taps_ref, skip_ref, mix_ref, out_ref):
    f32 = jnp.float32
    heads = mix_ref.shape[0]
    length = own_ref.shape[0]
    wide = own_ref.shape[1] // heads
    half = wide // 2
    first = lax.broadcasted_iota(jnp.int32, (length, wide), 1) < half
    kept = None
    for h in range(heads):
        columns = slice(h * wide, (h + 1) * wide)
        both = own_ref[:, columns] + away_ref[:, columns].astype(f32)
        conv = causal(both, taps_ref, columns)
        out = jnp.dot(mix_ref[h], conv, preferred_element_type=f32)
        out = out + skip_ref[:, h : h + 1] * conv.astype(f32)
        out = out * pltpu.roll(silu(both), half, 1)
        if h % 2 == 0:
            kept = pltpu.roll(out, half, 1)
        else:
            pair = jnp.where(first, kept, out).astype(jnp.bfloat16)
            for copy in range(out_ref.shape[0]):
                out_ref[copy, :, (h // 2) * wide : (h // 2 + 1) * wide] = pair


def pack(zx_weight, dt_weight, bc_weight, group_id, group_cols, columns):
    rows, heads, wide = zx_weight.shape
    start = heads * wide

    def kernel(group_ref, zx_ref, dt_ref, bc_ref, out_ref):
        for h in range(heads):
            out_ref[:, h * wide : (h + 1) * wide] = zx_ref[:, h, :]
        out_ref[:, start : start + group_cols] = bc_ref[...]
        last = start + group_cols
        out_ref[:, last:] = jnp.zeros((rows, columns - last), out_ref.dtype)
        out_ref[:, last : last + heads] = dt_ref[...]

    return pl.pallas_call(
        kernel,
        grid_spec=pltpu.PrefetchScalarGridSpec(
            num_scalar_prefetch=1,
            grid=(1,),
            in_specs=[
                pl.BlockSpec((rows, heads, wide), lambda i, group: (0, 0, 0)),
                pl.BlockSpec((rows, heads), lambda i, group: (0, 0)),
                pl.BlockSpec((rows, group_cols), lambda i, group: (0, group[0])),
            ],
            out_specs=pl.BlockSpec((rows, columns), lambda i, group: (0, 0)),
        ),
        out_shape=jax.ShapeDtypeStruct((rows, columns), zx_weight.dtype),
        name="pack",
    )(group_id[None], zx_weight, dt_weight, bc_weight)


def split_product(left, right, cut):
    rows, depth = left.shape
    columns = right.shape[1]
    step = depth // 4

    def kernel(left_ref, right_ref, first_ref, rest_ref, total_ref):
        @pl.when(pl.program_id(0) == 0)
        def _():
            total_ref[...] = jnp.zeros_like(total_ref)

        total_ref[...] += jnp.dot(left_ref[...], right_ref[...], preferred_element_type=jnp.float32)

        @pl.when(pl.program_id(0) == pl.num_programs(0) - 1)
        def _():
            first_ref[...] = total_ref[:, :cut].astype(first_ref.dtype)
            rest_ref[...] = total_ref[:, cut:].astype(rest_ref.dtype)

    return pl.pallas_call(
        kernel,
        grid=(depth // step,),
        in_specs=[
            pl.BlockSpec((rows, step), lambda k: (0, k)),
            pl.BlockSpec((step, columns), lambda k: (k, 0)),
        ],
        out_specs=[
            pl.BlockSpec((rows, cut), lambda k: (0, 0)),
            pl.BlockSpec((rows, columns - cut), lambda k: (0, 0)),
        ],
        out_shape=[
            jax.ShapeDtypeStruct((rows, cut), jnp.bfloat16),
            jax.ShapeDtypeStruct((rows, columns - cut), jnp.bfloat16),
        ],
        scratch_shapes=[pltpu.VMEM((rows, columns), jnp.float32)],
        cost_estimate=pl.CostEstimate(
            flops=2 * rows * depth * columns, bytes_accessed=2 * depth * columns, transcendentals=0
        ),
        name="split_product",
    )(left, right)


def on_chip(kernel, out_shape, flops, *args):
    moved = sum(a.size * a.dtype.itemsize for a in args) + 2 * out_shape.size
    return pl.pallas_call(
        kernel,
        out_shape=out_shape,
        cost_estimate=pl.CostEstimate(flops=flops, bytes_accessed=moved, transcendentals=0),
    )(*args)


def layer(
    tokens,
    zx_weight,
    dt_weight,
    bc_weight,
    conv_x,
    conv_bc,
    a_log,
    dt_bias,
    d_skip,
    norm_gain,
    out_weight,
):
    f32, bf16 = jnp.float32, jnp.bfloat16
    tok_rows = tokens.shape[0]
    _, heads_here, two_p = zx_weight.shape
    head_size = two_p // 2
    channels = heads_here * head_size
    n_yh, n_x = lax.axis_size("yh"), lax.axis_size("x")
    group_id = lax.axis_index("yh")
    group_cols = bc_weight.shape[1] // n_yh
    zx_cols = heads_here * two_p
    pad = -(zx_cols + group_cols + heads_here) % 128
    columns = zx_cols + group_cols + heads_here + pad
    mine = pack(zx_weight, dt_weight, bc_weight, group_id, group_cols, columns)
    k_half = lax.axis_index("yl")
    k_rows = tokens.shape[1] // 2
    kept = lax.dynamic_slice_in_dim(tokens, k_half * k_rows, k_rows, 1)
    given = lax.dynamic_slice_in_dim(tokens, (1 - k_half) * k_rows, k_rows, 1)
    given = lax.ppermute(given, "yl", SWAP)

    def padded(values):
        return jnp.pad(values, (0, 128 - heads_here))[None]

    conv_group = lax.dynamic_slice_in_dim(conv_bc, group_id * group_cols, group_cols, 1)
    taps = conv_x.shape[0]
    x_taps = conv_x.reshape(taps, heads_here, head_size)
    x_taps = jnp.concatenate([jnp.zeros_like(x_taps), x_taps], axis=2).reshape(taps, zx_cols)
    skips, rate, bias = padded(d_skip), padded(a_log), padded(dt_bias)

    whole = lax.all_gather(mine, ("z", "core"), axis=0, tiled=True)

    width = out_weight.shape[1] // (n_yh * n_x)
    pieces = repack(out_weight, norm_gain, n_yh, n_x)
    group_weight = lax.all_to_all(pieces, "x", 0, 0)
    group_weight = group_weight.reshape(n_x * channels, n_yh * width)

    ready = (whole, conv_group, x_taps, skips, rate, bias)
    whole, conv_group, x_taps, skips, rate, bias = lax.optimization_barrier(ready)

    def product(left, columns):
        return jnp.dot(left, whole[:, columns], preferred_element_type=f32)

    small, large = slice(zx_cols, None), slice(0, zx_cols)
    large_away, small_away = split_product(given, whole, zx_cols)
    small_away = lax.ppermute(small_away, "yl", SWAP)
    large_away = lax.ppermute(large_away, "yl", SWAP)
    small_own, large_own = product(kept, small), product(kept, large)
    mix = on_chip(
        mixing_kernel,
        jax.ShapeDtypeStruct((heads_here, tok_rows, tok_rows), bf16),
        10 * heads_here * tok_rows * tok_rows,
        small_own,
        small_away,
        conv_group,
        rate,
        bias,
    )
    mix, group_weight = lax.optimization_barrier((mix, group_weight))
    spread = on_chip(
        gated_kernel,
        jax.ShapeDtypeStruct((n_x, tok_rows, channels), bf16),
        4 * tok_rows * tok_rows * channels,
        large_own,
        large_away,
        x_taps,
        skips,
        mix,
    )
    group = lax.all_to_all(spread, "x", 0, 0)
    squares = jnp.sum(jnp.square(group.astype(f32)), axis=(0, 2))
    scale = lax.rsqrt(squares / (n_x * channels) + 1e-05)
    parts = jnp.einsum(
        "xtc,xcyw->ytw",
        group,
        group_weight.reshape(n_x, channels, n_yh, width),
        preferred_element_type=f32,
    )
    parts = (parts * scale[None, :, None]).astype(bf16)
    got = lax.all_to_all(parts, "yh", 0, 0)
    return jnp.sum(got.astype(f32), axis=0).astype(bf16)


def solution(mesh):
    fine = Mesh(mesh.devices.reshape(SIZES), FSDP + HEAD)
    in_specs = (
        P(FSDP, None),
        P(FSDP, HEAD, None),
        P(FSDP, HEAD),
        P(FSDP, None),
        P(None, HEAD),
        P(),
        P(HEAD),
        P(HEAD),
        P(HEAD),
        P(HEAD),
        P(HEAD, None),
    )
    return jax.shard_map(
        layer, mesh=fine, in_specs=in_specs, out_specs=P(FSDP, HEAD), check_vma=False
    )
```

```python
import jax
import jax.numpy as jnp
from jax import lax
from jax.experimental import pallas as pl
from jax.experimental.pallas import tpu as pltpu
from jax.sharding import Mesh, PartitionSpec as P

FSDP = ("yl", "z", "core")
HEAD = ("yh", "x")
SIZES = (2, 8, 2, 4, 8)
SWAP = [(0, 1), (1, 0)]


def repack(weight, gain, n_yh, n_x):
    rows, columns = weight.shape
    width = columns // (n_yh * n_x)

    step = rows // 8

    def kernel(gain_ref, weight_ref, out_ref):
        gains = gain_ref[...]
        for x in range(n_x):
            for y in range(n_yh):
                start = (y * n_x + x) * width
                value = weight_ref[:, start : start + width].astype(jnp.float32) * gains
                out_ref[x, :, y * width : (y + 1) * width] = value.astype(jnp.bfloat16)

    return pl.pallas_call(
        kernel,
        grid=(rows // step,),
        in_specs=[
            pl.BlockSpec((step, 1), lambda i: (i, 0)),
            pl.BlockSpec((step, columns), lambda i: (i, 0)),
        ],
        out_specs=pl.BlockSpec((n_x, step, n_yh * width), lambda i: (0, i, 0)),
        out_shape=jax.ShapeDtypeStruct((n_x, rows, n_yh * width), jnp.bfloat16),
        cost_estimate=pl.CostEstimate(
            flops=rows * columns, bytes_accessed=4 * rows * columns, transcendentals=0
        ),
        name="repack",
    )(gain[:, None], weight)


def silu(values):
    return values * jax.nn.sigmoid(values)


def causal(values, taps_ref, columns):
    rows = lax.broadcasted_iota(jnp.int32, values.shape, 0)
    n_taps = taps_ref.shape[0]
    total = taps_ref[n_taps - 1 : n_taps, columns] * values
    for back in range(1, n_taps):
        moved = jnp.where(rows >= back, pltpu.roll(values, back, 0), 0.0)
        total = total + taps_ref[n_taps - 1 - back : n_taps - back, columns] * moved
    return silu(total).astype(jnp.bfloat16)


def mixing_kernel(own_ref, away_ref, taps_ref, rate_ref, bias_ref, out_ref):
    f32 = jnp.float32
    heads, length, _ = out_ref.shape
    state = taps_ref.shape[1] // 2
    both = own_ref[...] + away_ref[...].astype(f32)
    keys = causal(both[:, :state], taps_ref, slice(0, state))
    queries = causal(both[:, state : 2 * state], taps_ref, slice(state, 2 * state))
    inner = lax.dot_general(queries, keys, (((1,), (1,)), ((), ())), preferred_element_type=f32)
    steps = jax.nn.softplus(both[:, 2 * state :] + bias_ref[...])
    rates = -steps * jnp.exp(rate_ref[...])
    shape = (length, length)
    lower = lax.broadcasted_iota(jnp.int32, shape, 0) >= lax.broadcasted_iota(jnp.int32, shape, 1)
    cum = jnp.dot(
        jnp.where(lower, 1.0, 0.0),
        rates,
        precision=lax.Precision.HIGHEST,
        preferred_element_type=f32,
    )
    cum_t, steps_t = cum.T, steps.T
    half = length // 2
    for h in range(heads):
        for rows, seen in ((slice(0, half), half), (slice(half, length), length)):
            seg = cum[rows, h : h + 1] - cum_t[h : h + 1, :seen]
            decay = jnp.exp(jnp.where(lower[rows, :seen], seg, -1e30))
            mixed = inner[rows, :seen] * decay * steps_t[h : h + 1, :seen]
            out_ref[h, rows, :seen] = mixed.astype(jnp.bfloat16)
        out_ref[h, :half, half:] = jnp.zeros((half, length - half), jnp.bfloat16)


def gated_kernel(own_ref, away_ref, taps_ref, skip_ref, mix_ref, out_ref):
    f32 = jnp.float32
    heads = mix_ref.shape[0]
    length = own_ref.shape[0]
    wide = own_ref.shape[1] // heads
    half = wide // 2
    first = lax.broadcasted_iota(jnp.int32, (length, wide), 1) < half
    kept = None
    for h in range(heads):
        columns = slice(h * wide, (h + 1) * wide)
        both = own_ref[:, columns] + away_ref[:, columns].astype(f32)
        conv = causal(both, taps_ref, columns)
        out = jnp.dot(mix_ref[h], conv, preferred_element_type=f32)
        out = out + skip_ref[:, h : h + 1] * conv.astype(f32)
        out = out * pltpu.roll(silu(both), half, 1)
        if h % 2 == 0:
            kept = pltpu.roll(out, half, 1)
        else:
            pair = jnp.where(first, kept, out).astype(jnp.bfloat16)
            for copy in range(out_ref.shape[0]):
                out_ref[copy, :, (h // 2) * wide : (h // 2 + 1) * wide] = pair


def on_chip(kernel, out_shape, flops, *args):
    moved = sum(a.size * a.dtype.itemsize for a in args) + 2 * out_shape.size
    return pl.pallas_call(
        kernel,
        out_shape=out_shape,
        cost_estimate=pl.CostEstimate(flops=flops, bytes_accessed=moved, transcendentals=0),
    )(*args)


def layer(
    tokens,
    zx_weight,
    dt_weight,
    bc_weight,
    conv_x,
    conv_bc,
    a_log,
    dt_bias,
    d_skip,
    norm_gain,
    out_weight,
):
    f32, bf16 = jnp.float32, jnp.bfloat16
    tok_rows = tokens.shape[0]
    rows, heads_here, two_p = zx_weight.shape
    head_size = two_p // 2
    channels = heads_here * head_size
    n_yh, n_x = lax.axis_size("yh"), lax.axis_size("x")
    group_id = lax.axis_index("yh")
    group_cols = bc_weight.shape[1] // n_yh
    bc_part = lax.dynamic_slice_in_dim(bc_weight, group_id * group_cols, group_cols, 1)
    zx_cols = heads_here * two_p
    pad = -(zx_cols + group_cols + heads_here) % 128
    mine = jnp.concatenate(
        [
            zx_weight.reshape(rows, zx_cols),
            bc_part,
            dt_weight,
            jnp.zeros((rows, pad), bf16),
        ],
        axis=1,
    )
    k_half = lax.axis_index("yl")
    k_rows = tokens.shape[1] // 2
    kept = lax.dynamic_slice_in_dim(tokens, k_half * k_rows, k_rows, 1)
    given = lax.dynamic_slice_in_dim(tokens, (1 - k_half) * k_rows, k_rows, 1)
    given = lax.ppermute(given, "yl", SWAP)

    def padded(values):
        return jnp.pad(values, (0, 128 - heads_here))[None]

    conv_group = lax.dynamic_slice_in_dim(conv_bc, group_id * group_cols, group_cols, 1)
    taps = conv_x.shape[0]
    x_taps = conv_x.reshape(taps, heads_here, head_size)
    x_taps = jnp.concatenate([jnp.zeros_like(x_taps), x_taps], axis=2).reshape(taps, zx_cols)
    skips, rate, bias = padded(d_skip), padded(a_log), padded(dt_bias)

    whole = lax.all_gather(mine, ("z", "core"), axis=0, tiled=True)

    width = out_weight.shape[1] // (n_yh * n_x)
    pieces = repack(out_weight, norm_gain, n_yh, n_x)
    group_weight = lax.all_to_all(pieces, "x", 0, 0)
    group_weight = group_weight.reshape(n_x * channels, n_yh * width)

    ready = (whole, conv_group, x_taps, skips, rate, bias)
    whole, conv_group, x_taps, skips, rate, bias = lax.optimization_barrier(ready)

    def product(left, columns):
        return jnp.dot(left, whole[:, columns], preferred_element_type=f32)

    small, large = slice(zx_cols, None), slice(0, zx_cols)
    small_away = lax.ppermute(product(given, small).astype(bf16), "yl", SWAP)
    large_away = lax.ppermute(product(given, large).astype(bf16), "yl", SWAP)
    small_own, large_own = product(kept, small), product(kept, large)
    mix = on_chip(
        mixing_kernel,
        jax.ShapeDtypeStruct((heads_here, tok_rows, tok_rows), bf16),
        10 * heads_here * tok_rows * tok_rows,
        small_own,
        small_away,
        conv_group,
        rate,
        bias,
    )
    mix, group_weight = lax.optimization_barrier((mix, group_weight))
    spread = on_chip(
        gated_kernel,
        jax.ShapeDtypeStruct((n_x, tok_rows, channels), bf16),
        4 * tok_rows * tok_rows * channels,
        large_own,
        large_away,
        x_taps,
        skips,
        mix,
    )
    group = lax.all_to_all(spread, "x", 0, 0)
    squares = jnp.sum(jnp.square(group.astype(f32)), axis=(0, 2))
    scale = lax.rsqrt(squares / (n_x * channels) + 1e-05)
    parts = jnp.einsum(
        "xtc,xcyw->ytw",
        group,
        group_weight.reshape(n_x, channels, n_yh, width),
        preferred_element_type=f32,
    )
    parts = (parts * scale[None, :, None]).astype(bf16)
    got = lax.all_to_all(parts, "yh", 0, 0)
    return jnp.sum(got.astype(f32), axis=0).astype(bf16)


def solution(mesh):
    fine = Mesh(mesh.devices.reshape(SIZES), FSDP + HEAD)
    in_specs = (
        P(FSDP, None),
        P(FSDP, HEAD, None),
        P(FSDP, HEAD),
        P(FSDP, None),
        P(None, HEAD),
        P(),
        P(HEAD),
        P(HEAD),
        P(HEAD),
        P(HEAD),
        P(HEAD, None),
    )
    return jax.shard_map(
        layer, mesh=fine, in_specs=in_specs, out_specs=P(FSDP, HEAD), check_vma=False
    )
```
